32 devices in a mesh: lsec: 4 (over y, x), rsec: 8 (over z, core).
Axes of the slice: x: 2, y: 2, z: 4, core: 2. Of those that a mesh axis runs over, the one named last changes fastest.
Arguments:
- psi: bfloat16 [16, 16, 256, 256], P('lsec', 'rsec'), may hold values from -6 to 6
- left_env: bfloat16 [16, 4, 256, 256], P('lsec'), may hold values from -0.375 to 0.375
- right_env: bfloat16 [16, 4, 256, 256], P('rsec'), may hold values from -0.1875 to 0.1875
- energies: float32 [16, 16], P('lsec', 'rsec'), may hold values from 0.5 to 3
- coef_num: int32 [2], replicated, may hold values from 3 to 9
- coef_den: int32 [2], replicated, may hold values from 4 to 8
Outputs:
- vector_out: bfloat16 [16, 16, 256, 256], P('lsec', 'rsec')
- ritz: float32 [3], replicated
The draws below stay inside these ranges and needn't reach their ends.
All inputs are finite; a program needn't handle non-finite values.
Results may differ from the reference program's by a relative error of at most 0.015.
Values may be sent and summed in bfloat16 or wider, within the bound.
A program may use at most 64 MiB of HBM per device.

```python
import jax
import jax.numpy as jnp
from jax import lax

B = 256
DIAG = 2
HOPS = 1
ITERS = 3
TERMS = 4
NA = 16
NB = 16


def block_levels(rng, dims, shards, smallest, top_value):
    loudness, own = 1.0, jax.random.fold_in(rng, 6)
    for dim, parts in shards:
        draws = jnp.exp(jax.random.uniform(jax.random.fold_in(own, dim), (parts,), jnp.float32, smallest / len(shards), top_value / len(shards)))
        loudness = loudness * jnp.repeat(draws, dims[dim] // parts).reshape([-1 if axis == dim else 1 for axis in range(len(dims))])
    return loudness


def centred(own_key, shape, width, bound, shards=(), kind=jnp.bfloat16):
    entries = jax.random.normal(own_key, shape, jnp.float32) * width
    if len(shards) > 0:
        entries = block_levels(own_key, shape, shards, -0.22, 0.18) * entries
    return jnp.clip(entries, min=-bound, max=bound).astype(kind)


def setup_inputs(seed: int = 0) -> dict:
    arg_keys = jax.random.split(jax.random.key(seed), 7)
    psi = centred(arg_keys[0], (NA, NB, B, B), 1.0, 6.0, ((0, 4), (1, 8)))
    left_env = centred(arg_keys[1], (NA, TERMS, B, B), B ** -0.5, 0.375, ((0, 4),))
    right_env = centred(arg_keys[2], (NB, TERMS, B, B), (B * TERMS) ** -0.5, 0.1875, ((0, 8),))
    energies = jnp.clip(0.5 + 2.5 * jax.random.uniform(arg_keys[3], (NA, NB), jnp.float32) ** block_levels(arg_keys[3], (NA, NB), ((0, 4), (1, 8)), -0.2, 0.2), 0.5, 3.0)
    coef_num = jax.random.randint(arg_keys[4], (ITERS - 1,), 3, 10).astype(jnp.int32)
    coef_den = jax.random.randint(arg_keys[5], (ITERS - 1,), 4, 9).astype(jnp.int32)
    return {"psi": psi, "left_env": left_env, "right_env": right_env, "energies": energies, "coef_num": coef_num, "coef_den": coef_den}


eps = 1e-06

def matvec(vec, left_env, right_env, energies):
    vals = vec.astype(jnp.float32)
    padded = jnp.pad(vals, ((1, 1), (1, 1), (0, 0), (0, 0)))
    plus_blocks = padded[:-2, 2:]
    minus_blocks = padded[2:, :-2]
    total = energies[:, :, None, None] * vals
    left_all = left_env.astype(jnp.float32)
    right_all = right_env.astype(jnp.float32)
    for term in range(DIAG + 2 * HOPS):
        if term < DIAG:
            source = vals
        elif term < DIAG + HOPS:
            source = plus_blocks
        else:
            source = minus_blocks
        inner = jnp.einsum('aij,abjk->abik', left_all[:, term], source).astype(jnp.bfloat16)
        total = total + jnp.einsum('abik,blk->abil', inner.astype(jnp.float32), right_all[:, term])
    return total

def reference(psi, left_env, right_env, energies, coef_num, coef_den):
    count = 1.0 / float(psi.size)
    start_vals = psi.astype(jnp.float32)
    start = jnp.sum(start_vals * start_vals) * count
    vec = (start_vals * lax.rsqrt(start + eps)).astype(jnp.bfloat16)
    previous = jnp.zeros(psi.shape, jnp.float32)
    thetas = []
    for step in range(ITERS):
        sigma = matvec(vec, left_env, right_env, energies)
        vals = vec.astype(jnp.float32)
        theta = jnp.sum(vals * sigma) * count
        thetas.append(theta)
        if step == 0:
            coef = jnp.float32(0.0)
        else:
            coef = coef_num[step - 1].astype(jnp.float32) / coef_den[step - 1].astype(jnp.float32)
        resid = sigma - theta * vals - coef * previous
        norm_sq = jnp.sum(resid * resid) * count
        previous = vals
        vec = (resid * lax.rsqrt(norm_sq + eps)).astype(jnp.bfloat16)
    return (vec, jnp.stack(thetas))
```

```python
import functools

import jax
import jax.numpy as jnp
from jax import lax
from jax.experimental import pallas as pl
from jax.experimental.pallas import tpu as pltpu
from jax.sharding import PartitionSpec as P

DIAG = 2
HOPS = 1
TERMS = DIAG + 2 * HOPS
ITERS = 3
eps = 1e-06
SHIFT = 1.75
GRAMS = 16
MESH = pl.DeviceIdType.MESH


def gram_row(i, j):
    return j * (j + 1) // 2 + i


def spans(nr):
    out = []
    while 2 ** len(out) < nr:
        out.append(2 ** len(out))
    return out


def kernel(
    nl, nr, count,
    psi, left_hbm, right_hbm, energies_hbm, num_hbm, den_hbm,
    ahead, prior, scalars,
    energies, coef_num, coef_den, q, stage_up, stage_dn, left, right, right_t, acc, local, early, late,
    in_sem, send_sem, recv_sem, token, esend, erecv, lsend, lrecv,
):
    na, nb, size, _ = psi.shape
    half = size // 2
    parts = nl * nr
    me_l, me_r = lax.axis_index("lsec"), lax.axis_index("rsec")
    me = me_l * nr + me_r
    lo_l, hi_l, lo_r, hi_r = me_l - 1, me_l + 1, me_r - 1, me_r + 1
    both, no = jnp.logical_and, jnp.logical_not
    has_lo_l, has_hi_l = me_l > 0, me_l < nl - 1
    has_lo_r, has_hi_r = me_r > 0, me_r < nr - 1
    up_dn, dn_up = both(has_hi_l, has_lo_r), both(has_lo_l, has_hi_r)
    odd = lax.rem(me_l, 2) == 1
    even = no(odd)
    via_hi = both(up_dn, both(odd, me_l + 2 < nl))
    via_lo = both(even, me_l >= 2)
    relay_up = both(both(odd, me_l >= 2), has_lo_r)
    relay_dn = both(even, me_l + 2 < nl)
    up_up = both(even, both(has_hi_l, has_hi_r))
    dn_dn = both(odd, has_lo_r)

    loads = [
        pltpu.make_async_copy(psi, q.at[0, 1 : na + 1, 1 : nb + 1], in_sem.at[0]),
        pltpu.make_async_copy(right_hbm, right, in_sem.at[1]),
        pltpu.make_async_copy(left_hbm, left, in_sem.at[2]),
    ]
    loads += [
        pltpu.make_async_copy(energies_hbm, energies, in_sem.at[3]),
        pltpu.make_async_copy(num_hbm, coef_num, in_sem.at[4]),
        pltpu.make_async_copy(den_hbm, coef_den, in_sem.at[5]),
    ]
    for load in loads:
        load.start()

    barrier = pltpu.get_barrier_semaphore()

    def greet(l, r):
        pl.semaphore_signal(barrier, inc=1, device_id=(l, r), device_id_type=MESH)

    partners = nl - 1
    for cond, l, r in (
        (has_lo_r, me_l, lo_r), (has_hi_r, me_l, hi_r),
        (up_dn, hi_l, lo_r), (dn_up, lo_l, hi_r),
        (up_up, hi_l, hi_r), (dn_dn, lo_l, lo_r),
    ):
        pl.when(cond)(lambda l=l, r=r: greet(l, r))
        partners = partners + cond.astype(jnp.int32)
    for step in range(1, nl):
        greet(lax.rem(me_l + step, nl), me_r)

    reach = spans(nr)

    def token_send(s):
        d = reach[s]
        for side, cond, r in ((0, me_r + d < nr, me_r + d), (1, me_r >= d, me_r - d)):
            pl.when(cond)(
                lambda side=side, r=r: pl.semaphore_signal(
                    token.at[s, side], inc=1, device_id=(me_l, r), device_id_type=MESH
                )
            )

    def token_wait(s):
        d = reach[s]
        for side, cond in ((0, me_r >= d), (1, me_r + d < nr)):
            pl.when(cond)(lambda side=side: pl.semaphore_wait(token.at[s, side], 1))

    def tokens(s):
        if s < len(reach):
            token_wait(s)
            if s + 1 < len(reach):
                token_send(s + 1)

    RP = 8
    RM = RP + na - 1

    def edges(k):
        here = q.at[k]
        own = psi if k == 0 else here.at[1 : na + 1, 1 : nb + 1]

        def rows(ref, h):
            lead = (slice(None),) * (len(ref.shape) - 2)
            return ref.at[lead + (pl.ds(h * half, half),)]

        out = {
            "U2": (has_hi_l, has_lo_l, own.at[na - 1, 1:nb], here.at[0, 2 : nb + 1], (hi_l, me_r), 0, 0),
            "U1": (both(up_dn, no(via_hi)), dn_up, own.at[na - 1, 0], here.at[0, nb + 1], (hi_l, lo_r), 1, 1),
            "D1": (both(has_lo_l, no(via_lo)), has_hi_l, own.at[0, 0 : nb - 1], here.at[na + 1, 1:nb], (lo_l, me_r), 2, 2),
            "D2": (dn_up, up_dn, own.at[0, nb - 1], here.at[na + 1, 0], (lo_l, hi_r), 3, 3),
        }
        for h in range(2):
            up, dn = rows(stage_up.at[k], h), rows(stage_dn.at[k], h)
            out[f"U1h{h}"] = (via_hi, relay_up, rows(own.at[na - 1, 0], h), up, (me_l + 2, me_r), 4 + h, 4 + h)
            out[f"D1h{h}"] = (via_lo, relay_dn, rows(own.at[0, 0 : nb - 1], h), dn, (me_l - 2, me_r), 6 + h, 6 + h)
            out[f"FU{h}"] = (relay_up, None, up, rows(here.at[0, nb + 1], h), (lo_l, lo_r), RM + na - 1 + h, 1)
            out[f"FD{h}"] = (relay_dn, None, dn, rows(here.at[na + 1, 1:nb], h), (hi_l, me_r), RM + na + 1 + h, 2)
        for i in range(1, na):
            n = RP + i - 1
            out[f"RP{i}"] = (has_lo_r, has_hi_r, own.at[i - 1, 0], here.at[i, nb + 1], (me_l, lo_r), n, n)
            n = RM + i - 1
            out[f"RM{i + 1}"] = (has_hi_r, has_lo_r, own.at[i, nb - 1], here.at[i + 1, 0], (me_l, hi_r), n, n)
        return out

    links = [edges(k) for k in range(ITERS)]

    def copy(k, name):
        _, _, src, dst, target, ssem, rsem = links[k][name]
        return pltpu.make_async_remote_copy(
            src_ref=src, dst_ref=dst,
            send_sem=send_sem.at[k, ssem], recv_sem=recv_sem.at[k, rsem],
            device_id=target, device_id_type=MESH,
        )

    def send(k, *names, when=None):
        if k < ITERS:
            for name in names:
                cond = links[k][name][0]
                cond = cond if when is None else both(cond, when)
                pl.when(cond)(lambda name=name: copy(k, name).start())

    def receive(k, *names, when=None):
        for name in names:
            cond = links[k][name][1]
            cond = cond if when is None else both(cond, when)
            pl.when(cond)(lambda name=name: copy(k, name).wait_recv())

    pl.semaphore_wait(barrier, partners)
    send(0, "U1h0", "D1h0", "U1h1", "D1h1", "U1", when=odd)
    send(0, "D1h0", "D1h1", when=even)
    send(0, "D1", when=odd)
    send(0, "U2", when=even)
    send(0, f"RP{na - 1}", "RM2")
    send(0, "U2", when=odd)
    send(0, "D2", "D1", when=even)
    rest_rp = [f"RP{i}" for i in range(na - 2, 0, -1)]
    rest_rm = [f"RM{i}" for i in range(3, na + 1)]
    send(0, *[name for pair in zip(rest_rp, rest_rm) for name in pair])
    token_send(0) if reach else None

    def clear(missing, slots):
        @pl.when(no(missing))
        def _():
            for k in range(ITERS):
                for i, j in slots:
                    q[k, i, j] = jnp.zeros((size, size), q.dtype)

    clear(has_lo_l, [(0, j) for j in range(2, nb + 1)])
    clear(dn_up, [(0, nb + 1)])
    clear(has_hi_l, [(na + 1, j) for j in range(1, nb)])
    clear(up_dn, [(na + 1, 0)])
    clear(has_hi_r, [(i, nb + 1) for i in range(1, na)])
    clear(has_lo_r, [(i, 0) for i in range(2, na + 1)])
    local[...] = jnp.zeros(local.shape, jnp.float32)

    def row(i):
        return jnp.where(odd, i, na + 1 - i)

    def col(j):
        return jnp.where(odd, j, nb + 1 - j)

    def shift(t):
        return 0 if t < DIAG else (1 if t < DIAG + HOPS else -1)

    def which(t):
        if t < DIAG:
            return t
        other = t + HOPS if t < DIAG + HOPS else t - HOPS
        return jnp.where(odd, t, other)

    def block(k, i, j):
        return q[k, row(i), col(j)]

    def term(k, i, j, t):
        source = block(k, i - shift(t), j + shift(t))
        inner = jnp.dot(left[row(i) - 1, which(t)], source, preferred_element_type=jnp.float32)
        return jnp.dot(
            inner.astype(jnp.bfloat16), right_t[col(j) - 1, which(t)],
            preferred_element_type=jnp.float32,
        )

    def is_local(i, j, t):
        return 1 <= i - shift(t) <= na and 1 <= j + shift(t) <= nb

    every = [(i, j) for i in range(1, na + 1) for j in range(1, nb + 1)]
    last = (1, nb)

    def begin(k, i, j, skip=None):
        total = (energies[col(j) - 1, row(i) - 1] - SHIFT) * block(k, i, j).astype(jnp.float32)
        for t in range(TERMS):
            if is_local(i, j, t) and (i - shift(t), j + shift(t)) != skip:
                total += term(k, i, j, t)
        acc[k % 2, row(i) - 1, col(j) - 1] = total

    def add(x, y, a, b):
        part = jnp.sum(x * y, axis=0, keepdims=True)
        at = pl.ds(gram_row(a, b), 1)
        for lane in range(0, size, 128):
            local[at, :] += part[:, lane : lane + 128]

    def grams(k, blocks):
        for i, j in blocks:
            new = block(k, i, j).astype(jnp.float32)
            for a in range(k + 1):
                add(block(a, i, j).astype(jnp.float32), new, a, k)

    def finish(k, i, j):
        total = acc[k % 2, row(i) - 1, col(j) - 1]
        for t in range(DIAG, TERMS):
            if not is_local(i, j, t):
                total += term(k, i, j, t)
        if k + 1 < ITERS:
            q[k + 1, row(i), col(j)] = total.astype(jnp.bfloat16)
        else:
            acc[k % 2, row(i) - 1, col(j) - 1] = total
            for a in range(ITERS):
                add(block(a, i, j).astype(jnp.float32), total, a, ITERS)
            add(total, total, ITERS, ITERS)

    def everyone(slots, ssem, rsem):
        def to(n):
            at = lax.rem(me + n, parts)
            return pltpu.make_async_remote_copy(
                src_ref=slots.at[me], dst_ref=slots.at[me], send_sem=ssem, recv_sem=rsem,
                device_id=(at // nr, lax.rem(at, nr)), device_id_type=MESH,
            )

        def begin():
            lax.fori_loop(1, parts, lambda n, c: (to(n).start(), c)[1], 0)

        whole = pltpu.make_async_remote_copy(
            src_ref=slots.at[0 : parts - 1], dst_ref=slots.at[0 : parts - 1],
            send_sem=ssem, recv_sem=rsem, device_id=(me_l, me_r), device_id_type=MESH,
        )
        return begin, whole

    def packed(first, size):
        totals = jnp.sum(local[...], axis=1, keepdims=True)
        place = lax.broadcasted_iota(jnp.int32, local.shape, 0)
        lanes = lax.broadcasted_iota(jnp.int32, local.shape, 1)
        return jnp.sum(jnp.where(place == lanes, totals, 0.0), axis=0, keepdims=True)

    early_begin, early_whole = everyone(early, esend, erecv)
    late_begin, late_whole = everyone(late, lsend, lrecv)

    loads[1].wait()
    for j in range(nb):
        for t in range(TERMS):
            right_t[j, t] = right[j, t].T
    for load in loads[:1] + loads[2:]:
        load.wait()
    for i, j in every:
        begin(0, i, j)
    grams(0, every)

    for k in range(ITERS):
        n = k + 1
        for h in range(2):
            receive(k, f"U1h{h}", f"D1h{h}")
            send(k, f"FU{h}", f"FD{h}")
        if k == 0:
            send(0, "D2", when=odd)
            send(0, "U1", when=even)

        receive(k, "U2", "RM2", when=odd)
        receive(k, "D1", f"RP{na - 1}", when=even)
        for j in range(1, nb):
            finish(k, 1, j)
        send(n, "D1", "RP1", when=odd)
        send(n, "U2", f"RM{na}", when=even)

        receive(k, *rest_rp, *rest_rm)
        inner = [(2, nb)] if na > 2 else []
        if na > 2:
            inner.append((na - 1, 1))
        for i, j in inner:
            finish(k, i, j)
        if na > 2:
            send(n, f"RP{na - 1}", "RM2")
        for i in range(2, na):
            for j in range(1, nb + 1):
                if (i, j) not in inner:
                    finish(k, i, j)
        send(n, *[f"RP{i}" for i in range(2, na - 1)], *[f"RM{i}" for i in range(3, na)])
        if k == 1:
            tokens(1)

        receive(k, "D1", f"RP{na - 1}", when=odd)
        receive(k, "U2", "RM2", when=even)
        for j in range(2, nb + 1):
            finish(k, na, j)
        send(n, "U2", f"RM{na}", when=odd)
        send(n, "D1h0", "D1h1", "D1", "RP1", when=even)

        receive(k, "D2", when=odd)
        receive(k, "U1", when=even)
        finish(k, na, 1)
        send(n, "U1h0", "U1h1", "U1", when=odd)
        send(n, "D2", when=even)

        if n < ITERS:
            ready = [b for b in every if b != last]
            for i, j in ready:
                begin(n, i, j, skip=last)
            grams(n, ready)

        receive(k, "U1", when=odd)
        receive(k, "D2", when=even)
        finish(k, *last)
        if n == ITERS - 1:
            for s in range(2, len(reach)):
                tokens(s)
            grams(n, [last])
            early[me] = packed(0, 0)
            early_begin()
        send(n, "D2", when=odd)
        send(n, "U1", when=even)
        if n < ITERS:
            begin(n, *last)
            if nb > 1:
                acc[n % 2, row(2) - 1, col(nb - 1) - 1] += term(n, 2, nb - 1, DIAG)
            if n < ITERS - 1:
                grams(n, [last])
        if k == 0:
            tokens(0)

    late[me] = packed(0, 0)
    late_begin()

    def plus(x, y):
        return y if x is None else (x if y is None else x + y)

    def scaled(s, x):
        return [None if part is None else s * part for part in x]

    def combine(*lists):
        return [functools.reduce(plus, parts) for parts in zip(*lists)]

    def product(x, y):
        total = jnp.zeros((1, 1), jnp.float32)
        for i in range(ITERS):
            for j in range(ITERS):
                if x[i] is not None and y[j] is not None:
                    at = gram_row(min(i, j), max(i, j))
                    total = total + x[i] * y[j] * sums[:, at : at + 1]
        return total

    early_whole.wait_recv()
    sums = jnp.sum(early[...], axis=0) * count
    vec = [lax.rsqrt(sums[:, 0:1] + eps)] + [None] * ITERS
    previous = None
    theta = []
    for k in range(ITERS):
        image = combine([None] + vec[:-1], scaled(SHIFT, vec))
        resid = image
        if k > 0:
            coef = jnp.full((1, 1), coef_num[k - 1].astype(jnp.float32)) / jnp.full(
                (1, 1), coef_den[k - 1].astype(jnp.float32)
            )
            resid = combine(resid, scaled(-coef, previous))
        if k + 1 == ITERS:
            break
        theta.append(product(vec, image))
        resid = combine(resid, scaled(-theta[k], vec))
        previous = vec
        vec = scaled(lax.rsqrt(product(resid, resid) + eps), resid)

    for i in range(na):
        for j in range(nb):
            new = acc[(ITERS - 1) % 2, i, j] * resid[ITERS]
            old = None
            for a in range(ITERS):
                part = q[a, i + 1, j + 1].astype(jnp.float32)
                new += part * resid[a]
                old = plus(old, part * vec[a])
            ahead[i, j] = new
            prior[i, j] = old

    theta_known = product(vec, image)
    both_known = product(resid, vec)
    new_known = product(resid, resid)
    old_known = product(vec, vec)
    early_whole.wait_send()
    for k in range(ITERS):
        for name, link in links[k].items():
            pl.when(link[0])(lambda k=k, name=name: copy(k, name).wait_send())

    late_whole.wait_recv()
    sums = jnp.sum(late[...], axis=0) * count

    def cross(x):
        total = jnp.zeros((1, 1), jnp.float32)
        for a in range(ITERS):
            at = gram_row(a, ITERS)
            total = total + x[a] * sums[:, at : at + 1]
        return total

    at = gram_row(ITERS, ITERS)
    top = resid[ITERS]
    with_vec = top * cross(vec)
    theta.append(theta_known + with_vec)
    overlap = both_known + with_vec
    square = new_known + top * (2.0 * cross(resid) + top * sums[:, at : at + 1])
    norm = square - theta[-1] * (2.0 * overlap - theta[-1] * old_known)
    scale = lax.rsqrt(norm + eps)
    values = [scale, scale * theta[-1]] + theta
    for n, value in enumerate(values):
        scalars[n : n + 1, :] = jnp.broadcast_to(value, (1, scalars.shape[1]))
    late_whole.wait_send()


def close(ahead, prior, scalars, out_hbm, ritz, out_v, sem):
    na, nb = ahead.shape[:2]
    scale, drop = scalars[0:1, 0:1], scalars[1:2, 0:1]
    stores = []
    for i in range(na):
        for j in range(nb):
            out_v[i, j] = (ahead[i, j] * scale - prior[i, j] * drop).astype(jnp.bfloat16)
        stores.append(pltpu.make_async_copy(out_v.at[i], out_hbm.at[i], sem.at[i]))
        stores[-1].start()
    for k in range(ITERS):
        ritz[k] = scalars[2 + k, 0]
    for store in stores:
        store.wait()


def per_device(nl, nr, psi, left_env, right_env, energies, coef_num, coef_den):
    na, nb, size, _ = psi.shape
    count = 1.0 / float(psi.size * nl * nr)
    hbm = pl.BlockSpec(memory_space=pltpu.HBM)
    smem = pl.BlockSpec(memory_space=pltpu.SMEM)
    vmem = pl.BlockSpec(memory_space=pltpu.VMEM)
    dma = pltpu.SemaphoreType.DMA
    flows = 12 + 2 * (na - 1)
    ahead, prior, scalars = pl.pallas_call(
        functools.partial(kernel, nl, nr, count),
        out_shape=(
            pltpu.VMEM(psi.shape, jnp.float32),
            pltpu.VMEM(psi.shape, jnp.float32),
            pltpu.VMEM((8, 128), jnp.float32),
        ),
        in_specs=[hbm] * 6,
        out_specs=(vmem, vmem, vmem),
        scratch_shapes=[
            pltpu.SMEM((nb, na), jnp.float32),
            pltpu.SMEM(coef_num.shape, jnp.int32),
            pltpu.SMEM(coef_den.shape, jnp.int32),
            pltpu.VMEM((ITERS, na + 2, nb + 2, size, size), jnp.bfloat16),
            pltpu.VMEM((ITERS, size, size), jnp.bfloat16),
            pltpu.VMEM((ITERS, nb - 1, size, size), jnp.bfloat16),
            pltpu.VMEM(left_env.shape, jnp.bfloat16),
            pltpu.VMEM(right_env.shape, jnp.bfloat16),
            pltpu.VMEM(right_env.shape, jnp.bfloat16),
            pltpu.VMEM((2,) + psi.shape, jnp.float32),
            pltpu.VMEM((GRAMS, 128), jnp.float32),
            pltpu.VMEM((nl * nr, 1, 128), jnp.float32),
            pltpu.VMEM((nl * nr, 1, 128), jnp.float32),
            dma((6,)),
            dma((ITERS, flows)),
            dma((ITERS, flows)),
            pltpu.SemaphoreType.REGULAR((max(1, len(spans(nr))), 2)),
            dma, dma, dma, dma,
        ],
        compiler_params=pltpu.CompilerParams(
            collective_id=0, has_side_effects=True, vmem_limit_bytes=52000000
        ),
    )(psi, left_env, right_env, energies.T, coef_num, coef_den)
    return pl.pallas_call(
        close,
        out_shape=(
            jax.ShapeDtypeStruct(psi.shape, jnp.bfloat16),
            jax.ShapeDtypeStruct((ITERS,), jnp.float32),
        ),
        in_specs=[vmem] * 3,
        out_specs=(hbm, smem),
        scratch_shapes=[pltpu.VMEM(psi.shape, jnp.bfloat16), dma((na,))],
        compiler_params=pltpu.CompilerParams(vmem_limit_bytes=8000000),
    )(ahead, prior, scalars)


def solution(mesh):
    in_specs = (
        P("lsec", "rsec", None, None),
        P("lsec", None, None, None),
        P("rsec", None, None, None),
        P("lsec", "rsec"),
        P(),
        P(),
    )
    out_specs = (P("lsec", "rsec", None, None), P())
    body = functools.partial(per_device, mesh.shape["lsec"], mesh.shape["rsec"])
    return jax.shard_map(
        body, mesh=mesh, in_specs=in_specs, out_specs=out_specs, check_vma=False
    )
```

```python
import functools

import jax
import jax.numpy as jnp
from jax import lax
from jax.experimental import pallas as pl
from jax.experimental.pallas import tpu as pltpu
from jax.sharding import PartitionSpec as P

DIAG = 2
HOPS = 1
TERMS = DIAG + 2 * HOPS
ITERS = 3
eps = 1e-06
SHIFT = 1.75
GRAMS = 16
MESH = pl.DeviceIdType.MESH


def gram_row(i, j):
    return j * (j + 1) // 2 + i


def spans(nr):
    out = []
    while 2 ** len(out) < nr:
        out.append(2 ** len(out))
    return out


def kernel(
    nl, nr, count,
    psi, left_hbm, right_hbm, energies_hbm, num_hbm, den_hbm,
    ahead, prior, scalars,
    energies, coef_num, coef_den, q, stage_up, stage_dn, left, right, right_t, acc, local, early, late,
    in_sem, send_sem, recv_sem, token, esend, erecv, lsend, lrecv,
):
    na, nb, size, _ = psi.shape
    half = size // 2
    parts = nl * nr
    me_l, me_r = lax.axis_index("lsec"), lax.axis_index("rsec")
    me = me_l * nr + me_r
    lo_l, hi_l, lo_r, hi_r = me_l - 1, me_l + 1, me_r - 1, me_r + 1
    both, no = jnp.logical_and, jnp.logical_not
    has_lo_l, has_hi_l = me_l > 0, me_l < nl - 1
    has_lo_r, has_hi_r = me_r > 0, me_r < nr - 1
    up_dn, dn_up = both(has_hi_l, has_lo_r), both(has_lo_l, has_hi_r)
    odd = lax.rem(me_l, 2) == 1
    even = no(odd)
    via_hi = both(up_dn, both(odd, me_l + 2 < nl))
    via_lo = both(even, me_l >= 2)
    relay_up = both(both(odd, me_l >= 2), has_lo_r)
    relay_dn = both(even, me_l + 2 < nl)
    up_up = both(even, both(has_hi_l, has_hi_r))
    dn_dn = both(odd, has_lo_r)

    loads = [
        pltpu.make_async_copy(psi, q.at[0, 1 : na + 1, 1 : nb + 1], in_sem.at[0]),
        pltpu.make_async_copy(right_hbm, right, in_sem.at[1]),
        pltpu.make_async_copy(left_hbm, left, in_sem.at[2]),
    ]
    loads += [
        pltpu.make_async_copy(energies_hbm, energies, in_sem.at[3]),
        pltpu.make_async_copy(num_hbm, coef_num, in_sem.at[4]),
        pltpu.make_async_copy(den_hbm, coef_den, in_sem.at[5]),
    ]
    for load in loads:
        load.start()

    barrier = pltpu.get_barrier_semaphore()

    def greet(l, r):
        pl.semaphore_signal(barrier, inc=1, device_id=(l, r), device_id_type=MESH)

    partners = nl - 1
    for cond, l, r in (
        (has_lo_r, me_l, lo_r), (has_hi_r, me_l, hi_r),
        (up_dn, hi_l, lo_r), (dn_up, lo_l, hi_r),
        (up_up, hi_l, hi_r), (dn_dn, lo_l, lo_r),
    ):
        pl.when(cond)(lambda l=l, r=r: greet(l, r))
        partners = partners + cond.astype(jnp.int32)
    for step in range(1, nl):
        greet(lax.rem(me_l + step, nl), me_r)

    reach = spans(nr)

    def token_send(s):
        d = reach[s]
        for side, cond, r in ((0, me_r + d < nr, me_r + d), (1, me_r >= d, me_r - d)):
            pl.when(cond)(
                lambda side=side, r=r: pl.semaphore_signal(
                    token.at[s, side], inc=1, device_id=(me_l, r), device_id_type=MESH
                )
            )

    def token_wait(s):
        d = reach[s]
        for side, cond in ((0, me_r >= d), (1, me_r + d < nr)):
            pl.when(cond)(lambda side=side: pl.semaphore_wait(token.at[s, side], 1))

    def tokens(s):
        if s < len(reach):
            token_wait(s)
            if s + 1 < len(reach):
                token_send(s + 1)

    RP = 8
    RM = RP + na - 1

    def edges(k):
        here = q.at[k]
        own = psi if k == 0 else here.at[1 : na + 1, 1 : nb + 1]

        def rows(ref, h):
            lead = (slice(None),) * (len(ref.shape) - 2)
            return ref.at[lead + (pl.ds(h * half, half),)]

        out = {
            "U2": (has_hi_l, has_lo_l, own.at[na - 1, 1:nb], here.at[0, 2 : nb + 1], (hi_l, me_r), 0, 0),
            "U1": (both(up_dn, no(via_hi)), dn_up, own.at[na - 1, 0], here.at[0, nb + 1], (hi_l, lo_r), 1, 1),
            "D1": (both(has_lo_l, no(via_lo)), has_hi_l, own.at[0, 0 : nb - 1], here.at[na + 1, 1:nb], (lo_l, me_r), 2, 2),
            "D2": (dn_up, up_dn, own.at[0, nb - 1], here.at[na + 1, 0], (lo_l, hi_r), 3, 3),
        }
        for h in range(2):
            up, dn = rows(stage_up.at[k], h), rows(stage_dn.at[k], h)
            out[f"U1h{h}"] = (via_hi, relay_up, rows(own.at[na - 1, 0], h), up, (me_l + 2, me_r), 4 + h, 4 + h)
            out[f"D1h{h}"] = (via_lo, relay_dn, rows(own.at[0, 0 : nb - 1], h), dn, (me_l - 2, me_r), 6 + h, 6 + h)
            out[f"FU{h}"] = (relay_up, None, up, rows(here.at[0, nb + 1], h), (lo_l, lo_r), RM + na - 1 + h, 1)
            out[f"FD{h}"] = (relay_dn, None, dn, rows(here.at[na + 1, 1:nb], h), (hi_l, me_r), RM + na + 1 + h, 2)
        for i in range(1, na):
            n = RP + i - 1
            out[f"RP{i}"] = (has_lo_r, has_hi_r, own.at[i - 1, 0], here.at[i, nb + 1], (me_l, lo_r), n, n)
            n = RM + i - 1
            out[f"RM{i + 1}"] = (has_hi_r, has_lo_r, own.at[i, nb - 1], here.at[i + 1, 0], (me_l, hi_r), n, n)
        return out

    links = [edges(k) for k in range(ITERS)]

    def copy(k, name):
        _, _, src, dst, target, ssem, rsem = links[k][name]
        return pltpu.make_async_remote_copy(
            src_ref=src, dst_ref=dst,
            send_sem=send_sem.at[k, ssem], recv_sem=recv_sem.at[k, rsem],
            device_id=target, device_id_type=MESH,
        )

    def send(k, *names, when=None):
        if k < ITERS:
            for name in names:
                cond = links[k][name][0]
                cond = cond if when is None else both(cond, when)
                pl.when(cond)(lambda name=name: copy(k, name).start())

    def receive(k, *names, when=None):
        for name in names:
            cond = links[k][name][1]
            cond = cond if when is None else both(cond, when)
            pl.when(cond)(lambda name=name: copy(k, name).wait_recv())

    pl.semaphore_wait(barrier, partners)
    send(0, "U1h0", "D1h0", "U1h1", "D1h1", "U1", when=odd)
    send(0, "D1h0", "D1h1", when=even)
    send(0, "D1", when=odd)
    send(0, "U2", when=even)
    send(0, f"RP{na - 1}", "RM2")
    send(0, "U2", when=odd)
    send(0, "D2", "D1", when=even)
    rest_rp = [f"RP{i}" for i in range(na - 2, 0, -1)]
    rest_rm = [f"RM{i}" for i in range(3, na + 1)]
    send(0, *[name for pair in zip(rest_rp, rest_rm) for name in pair])
    token_send(0) if reach else None

    def clear(missing, slots):
        @pl.when(no(missing))
        def _():
            for k in range(ITERS):
                for i, j in slots:
                    q[k, i, j] = jnp.zeros((size, size), q.dtype)

    def row(i):
        return jnp.where(odd, i, na + 1 - i)

    def col(j):
        return jnp.where(odd, j, nb + 1 - j)

    def shift(t):
        return 0 if t < DIAG else (1 if t < DIAG + HOPS else -1)

    def which(t):
        if t < DIAG:
            return t
        other = t + HOPS if t < DIAG + HOPS else t - HOPS
        return jnp.where(odd, t, other)

    def block(k, i, j):
        return q[k, row(i), col(j)]

    def term(k, i, j, t):
        source = block(k, i - shift(t), j + shift(t))
        inner = jnp.dot(left[row(i) - 1, which(t)], source, preferred_element_type=jnp.float32)
        return jnp.dot(
            inner.astype(jnp.bfloat16), right_t[col(j) - 1, which(t)],
            preferred_element_type=jnp.float32,
        )

    def is_local(i, j, t):
        return 1 <= i - shift(t) <= na and 1 <= j + shift(t) <= nb

    every = [(i, j) for i in range(1, na + 1) for j in range(1, nb + 1)]
    last = (1, nb)

    def begin(k, i, j, skip=None, only=False, fresh=True):
        if fresh:
            total = (energies[col(j) - 1, row(i) - 1] - SHIFT) * block(k, i, j).astype(jnp.float32)
        else:
            total = acc[k % 2, row(i) - 1, col(j) - 1]
        for t in range(TERMS):
            if only and t >= DIAG or not fresh and t < DIAG:
                continue
            if is_local(i, j, t) and (i - shift(t), j + shift(t)) != skip:
                total += term(k, i, j, t)
        acc[k % 2, row(i) - 1, col(j) - 1] = total

    def add(x, y, a, b):
        part = jnp.sum(x * y, axis=0, keepdims=True)
        at = pl.ds(gram_row(a, b), 1)
        for lane in range(0, size, 128):
            local[at, :] += part[:, lane : lane + 128]

    def grams(k, blocks):
        for i, j in blocks:
            new = block(k, i, j).astype(jnp.float32)
            for a in range(k + 1):
                add(block(a, i, j).astype(jnp.float32), new, a, k)

    def finish(k, i, j):
        total = acc[k % 2, row(i) - 1, col(j) - 1]
        for t in range(DIAG, TERMS):
            if not is_local(i, j, t):
                total += term(k, i, j, t)
        if k + 1 < ITERS:
            q[k + 1, row(i), col(j)] = total.astype(jnp.bfloat16)
        else:
            acc[k % 2, row(i) - 1, col(j) - 1] = total
            for a in range(ITERS):
                add(block(a, i, j).astype(jnp.float32), total, a, ITERS)
            add(total, total, ITERS, ITERS)

    def everyone(slots, ssem, rsem):
        def to(n):
            at = lax.rem(me + n, parts)
            return pltpu.make_async_remote_copy(
                src_ref=slots.at[me], dst_ref=slots.at[me], send_sem=ssem, recv_sem=rsem,
                device_id=(at // nr, lax.rem(at, nr)), device_id_type=MESH,
            )

        def begin():
            lax.fori_loop(1, parts, lambda n, c: (to(n).start(), c)[1], 0)

        whole = pltpu.make_async_remote_copy(
            src_ref=slots.at[0 : parts - 1], dst_ref=slots.at[0 : parts - 1],
            send_sem=ssem, recv_sem=rsem, device_id=(me_l, me_r), device_id_type=MESH,
        )
        return begin, whole

    def packed(first, size):
        totals = jnp.sum(local[...], axis=1, keepdims=True)
        place = lax.broadcasted_iota(jnp.int32, local.shape, 0)
        lanes = lax.broadcasted_iota(jnp.int32, local.shape, 1)
        return jnp.sum(jnp.where(place == lanes, totals, 0.0), axis=0, keepdims=True)

    early_begin, early_whole = everyone(early, esend, erecv)
    late_begin, late_whole = everyone(late, lsend, lrecv)

    def forward(k, h):
        receive(k, f"U1h{h}", f"D1h{h}")
        send(k, f"FU{h}", f"FD{h}")

    loads[1].wait()
    for j in range(nb):
        for t in range(TERMS):
            right_t[j, t] = right[j, t].T
    for load in loads[:1] + loads[2:]:
        load.wait()
    forward(0, 0)
    for j in range(1, nb):
        begin(0, 1, j)
    forward(0, 1)
    send(0, "D2", when=odd)
    send(0, "U1", when=even)
    clear(has_lo_l, [(0, j) for j in range(2, nb + 1)])
    clear(dn_up, [(0, nb + 1)])
    clear(has_hi_l, [(na + 1, j) for j in range(1, nb)])
    clear(up_dn, [(na + 1, 0)])
    clear(has_hi_r, [(i, nb + 1) for i in range(1, na)])
    clear(has_lo_r, [(i, 0) for i in range(2, na + 1)])
    local[...] = jnp.zeros(local.shape, jnp.float32)
    for k in range(ITERS):
        n = k + 1
        if k > 0:
            for h in range(2):
                forward(k, h)

        receive(k, "U2", "RM2", when=odd)
        receive(k, "D1", f"RP{na - 1}", when=even)
        for j in range(1, nb):
            finish(k, 1, j)
        send(n, "D1", "RP1", when=odd)
        send(n, "U2", f"RM{na}", when=even)

        if k == 0:
            for i, j in every:
                if i > 1 or j == nb:
                    begin(0, i, j)
        receive(k, *rest_rp, *rest_rm)
        inner = [(2, nb)] if na > 2 else []
        if na > 2:
            inner.append((na - 1, 1))
        for i, j in inner:
            finish(k, i, j)
        if na > 2:
            send(n, f"RP{na - 1}", "RM2")
        for i in range(2, na):
            for j in range(1, nb + 1):
                if (i, j) not in inner:
                    finish(k, i, j)
        send(n, *[f"RP{i}" for i in range(2, na - 1)], *[f"RM{i}" for i in range(3, na)])
        if k == 1:
            tokens(1)
        if n < ITERS:
            for i in range(2, na):
                for j in range(1, nb + 1):
                    begin(n, i, j, only=True)
            grams(n, [(i, j) for i in range(1, na) for j in range(1, nb + 1) if (i, j) != last])

        if k == 0:
            grams(0, every)
        receive(k, "D1", f"RP{na - 1}", when=odd)
        receive(k, "U2", "RM2", when=even)
        for j in range(2, nb + 1):
            finish(k, na, j)
        send(n, "U2", f"RM{na}", when=odd)
        send(n, "D1h0", "D1h1", "D1", "RP1", when=even)

        receive(k, "D2", when=odd)
        receive(k, "U1", when=even)
        finish(k, na, 1)
        send(n, "U1h0", "U1h1", "U1", when=odd)
        send(n, "D2", when=even)

        if n < ITERS:
            for i, j in every:
                if 1 < i < na:
                    begin(n, i, j, skip=last, fresh=False)
                elif (i, j) != last:
                    begin(n, i, j, skip=last)
            grams(n, [(na, j) for j in range(1, nb + 1)])

        receive(k, "U1", when=odd)
        receive(k, "D2", when=even)
        finish(k, *last)
        if n == ITERS - 1:
            for s in range(2, len(reach)):
                tokens(s)
            grams(n, [last])
            early[me] = packed(0, 0)
            early_begin()
        send(n, "D2", when=odd)
        send(n, "U1", when=even)
        if n < ITERS:
            begin(n, *last)
            if nb > 1:
                acc[n % 2, row(2) - 1, col(nb - 1) - 1] += term(n, 2, nb - 1, DIAG)
            if n < ITERS - 1:
                grams(n, [last])
        if k == 0:
            tokens(0)

    late[me] = packed(0, 0)
    late_begin()

    def plus(x, y):
        return y if x is None else (x if y is None else x + y)

    def scaled(s, x):
        return [None if part is None else s * part for part in x]

    def combine(*lists):
        return [functools.reduce(plus, parts) for parts in zip(*lists)]

    def product(x, y):
        total = jnp.zeros((1, 1), jnp.float32)
        for i in range(ITERS):
            for j in range(ITERS):
                if x[i] is not None and y[j] is not None:
                    at = gram_row(min(i, j), max(i, j))
                    total = total + x[i] * y[j] * sums[:, at : at + 1]
        return total

    early_whole.wait_recv()
    sums = jnp.sum(early[...], axis=0) * count
    vec = [lax.rsqrt(sums[:, 0:1] + eps)] + [None] * ITERS
    previous = None
    theta = []
    for k in range(ITERS):
        image = combine([None] + vec[:-1], scaled(SHIFT, vec))
        resid = image
        if k > 0:
            coef = jnp.full((1, 1), coef_num[k - 1].astype(jnp.float32)) / jnp.full(
                (1, 1), coef_den[k - 1].astype(jnp.float32)
            )
            resid = combine(resid, scaled(-coef, previous))
        if k + 1 == ITERS:
            break
        theta.append(product(vec, image))
        resid = combine(resid, scaled(-theta[k], vec))
        previous = vec
        vec = scaled(lax.rsqrt(product(resid, resid) + eps), resid)

    for i in range(na):
        for j in range(nb):
            new = acc[(ITERS - 1) % 2, i, j] * resid[ITERS]
            old = None
            for a in range(ITERS):
                part = q[a, i + 1, j + 1].astype(jnp.float32)
                new += part * resid[a]
                old = plus(old, part * vec[a])
            ahead[i, j] = new
            prior[i, j] = old

    theta_known = product(vec, image)
    both_known = product(resid, vec)
    new_known = product(resid, resid)
    old_known = product(vec, vec)
    early_whole.wait_send()
    for k in range(ITERS):
        for name, link in links[k].items():
            pl.when(link[0])(lambda k=k, name=name: copy(k, name).wait_send())

    late_whole.wait_recv()
    sums = jnp.sum(late[...], axis=0) * count

    def cross(x):
        total = jnp.zeros((1, 1), jnp.float32)
        for a in range(ITERS):
            at = gram_row(a, ITERS)
            total = total + x[a] * sums[:, at : at + 1]
        return total

    at = gram_row(ITERS, ITERS)
    top = resid[ITERS]
    with_vec = top * cross(vec)
    theta.append(theta_known + with_vec)
    overlap = both_known + with_vec
    square = new_known + top * (2.0 * cross(resid) + top * sums[:, at : at + 1])
    norm = square - theta[-1] * (2.0 * overlap - theta[-1] * old_known)
    scale = lax.rsqrt(norm + eps)
    values = [scale, scale * theta[-1]] + theta
    for n, value in enumerate(values):
        scalars[n : n + 1, :] = jnp.broadcast_to(value, (1, scalars.shape[1]))
    late_whole.wait_send()


def close(ahead, prior, scalars, out_hbm, ritz, out_v, sem):
    na, nb = ahead.shape[:2]
    scale, drop = scalars[0:1, 0:1], scalars[1:2, 0:1]
    stores = []
    for i in range(na):
        for j in range(nb):
            out_v[i, j] = (ahead[i, j] * scale - prior[i, j] * drop).astype(jnp.bfloat16)
            stores.append(pltpu.make_async_copy(out_v.at[i, j], out_hbm.at[i, j], sem.at[i, j]))
            stores[-1].start()
    for k in range(ITERS):
        ritz[k] = scalars[2 + k, 0]
    for store in stores:
        store.wait()


def per_device(nl, nr, psi, left_env, right_env, energies, coef_num, coef_den):
    na, nb, size, _ = psi.shape
    count = 1.0 / float(psi.size * nl * nr)
    hbm = pl.BlockSpec(memory_space=pltpu.HBM)
    smem = pl.BlockSpec(memory_space=pltpu.SMEM)
    vmem = pl.BlockSpec(memory_space=pltpu.VMEM)
    dma = pltpu.SemaphoreType.DMA
    flows = 12 + 2 * (na - 1)
    ahead, prior, scalars = pl.pallas_call(
        functools.partial(kernel, nl, nr, count),
        out_shape=(
            pltpu.VMEM(psi.shape, jnp.float32),
            pltpu.VMEM(psi.shape, jnp.float32),
            pltpu.VMEM((8, 128), jnp.float32),
        ),
        in_specs=[hbm] * 6,
        out_specs=(vmem, vmem, vmem),
        scratch_shapes=[
            pltpu.SMEM((nb, na), jnp.float32),
            pltpu.SMEM(coef_num.shape, jnp.int32),
            pltpu.SMEM(coef_den.shape, jnp.int32),
            pltpu.VMEM((ITERS, na + 2, nb + 2, size, size), jnp.bfloat16),
            pltpu.VMEM((ITERS, size, size), jnp.bfloat16),
            pltpu.VMEM((ITERS, nb - 1, size, size), jnp.bfloat16),
            pltpu.VMEM(left_env.shape, jnp.bfloat16),
            pltpu.VMEM(right_env.shape, jnp.bfloat16),
            pltpu.VMEM(right_env.shape, jnp.bfloat16),
            pltpu.VMEM((2,) + psi.shape, jnp.float32),
            pltpu.VMEM((GRAMS, 128), jnp.float32),
            pltpu.VMEM((nl * nr, 1, 128), jnp.float32),
            pltpu.VMEM((nl * nr, 1, 128), jnp.float32),
            dma((6,)),
            dma((ITERS, flows)),
            dma((ITERS, flows)),
            pltpu.SemaphoreType.REGULAR((max(1, len(spans(nr))), 2)),
            dma, dma, dma, dma,
        ],
        compiler_params=pltpu.CompilerParams(
            collective_id=0, has_side_effects=True, vmem_limit_bytes=60000000
        ),
    )(psi, left_env, right_env, energies.T, coef_num, coef_den)
    return pl.pallas_call(
        close,
        out_shape=(
            jax.ShapeDtypeStruct(psi.shape, jnp.bfloat16),
            jax.ShapeDtypeStruct((ITERS,), jnp.float32),
        ),
        in_specs=[vmem] * 3,
        out_specs=(hbm, smem),
        scratch_shapes=[pltpu.VMEM(psi.shape, jnp.bfloat16), dma((na, nb))],
        compiler_params=pltpu.CompilerParams(vmem_limit_bytes=8000000),
    )(ahead, prior, scalars)


def solution(mesh):
    in_specs = (
        P("lsec", "rsec", None, None),
        P("lsec", None, None, None),
        P("rsec", None, None, None),
        P("lsec", "rsec"),
        P(),
        P(),
    )
    out_specs = (P("lsec", "rsec", None, None), P())
    body = functools.partial(per_device, mesh.shape["lsec"], mesh.shape["rsec"])
    return jax.shard_map(
        body, mesh=mesh, in_specs=in_specs, out_specs=out_specs, check_vma=False
    )
```

```python
import functools

import jax
import jax.numpy as jnp
from jax import lax
from jax.experimental import pallas as pl
from jax.experimental.pallas import tpu as pltpu
from jax.sharding import PartitionSpec as P

DIAG = 2
HOPS = 1
TERMS = DIAG + 2 * HOPS
ITERS = 3
eps = 1e-06
SHIFT = 1.75
GRAMS = 16
MESH = pl.DeviceIdType.MESH


def gram_row(i, j):
    return j * (j + 1) // 2 + i


def spans(nr):
    out = []
    while 2 ** len(out) < nr:
        out.append(2 ** len(out))
    return out


def kernel(
    nl, nr, count,
    psi, left_hbm, right_hbm, energies_hbm, num_hbm, den_hbm,
    ahead, prior, scalars,
    energies, coef_num, coef_den, q, stage_up, stage_dn, left, right, right_t, acc, local, early, late,
    in_sem, send_sem, recv_sem, token, esend, erecv, lsend, lrecv,
):
    na, nb, size, _ = psi.shape
    half = size // 2
    parts = nl * nr
    me_l, me_r = lax.axis_index("lsec"), lax.axis_index("rsec")
    me = me_l * nr + me_r
    lo_l, hi_l, lo_r, hi_r = me_l - 1, me_l + 1, me_r - 1, me_r + 1
    both, no = jnp.logical_and, jnp.logical_not
    has_lo_l, has_hi_l = me_l > 0, me_l < nl - 1
    has_lo_r, has_hi_r = me_r > 0, me_r < nr - 1
    up_dn, dn_up = both(has_hi_l, has_lo_r), both(has_lo_l, has_hi_r)
    odd = lax.rem(me_l, 2) == 1
    even = no(odd)
    via_hi = both(up_dn, both(odd, me_l + 2 < nl))
    via_lo = both(even, me_l >= 2)
    relay_up = both(both(odd, me_l >= 2), has_lo_r)
    relay_dn = both(even, me_l + 2 < nl)
    up_up = both(even, both(has_hi_l, has_hi_r))
    dn_dn = both(odd, has_lo_r)

    loads = [
        pltpu.make_async_copy(psi, q.at[0, 1 : na + 1, 1 : nb + 1], in_sem.at[0]),
        pltpu.make_async_copy(right_hbm, right, in_sem.at[1]),
        pltpu.make_async_copy(left_hbm, left, in_sem.at[2]),
    ]
    loads += [
        pltpu.make_async_copy(energies_hbm, energies, in_sem.at[3]),
        pltpu.make_async_copy(num_hbm, coef_num, in_sem.at[4]),
        pltpu.make_async_copy(den_hbm, coef_den, in_sem.at[5]),
    ]
    for load in loads:
        load.start()

    barrier = pltpu.get_barrier_semaphore()

    def greet(l, r):
        pl.semaphore_signal(barrier, inc=1, device_id=(l, r), device_id_type=MESH)

    partners = nl - 1
    for cond, l, r in (
        (has_lo_r, me_l, lo_r), (has_hi_r, me_l, hi_r),
        (up_dn, hi_l, lo_r), (dn_up, lo_l, hi_r),
        (up_up, hi_l, hi_r), (dn_dn, lo_l, lo_r),
    ):
        pl.when(cond)(lambda l=l, r=r: greet(l, r))
        partners = partners + cond.astype(jnp.int32)
    for step in range(1, nl):
        greet(lax.rem(me_l + step, nl), me_r)

    reach = spans(nr)

    def token_send(s):
        d = reach[s]
        for side, cond, r in ((0, me_r + d < nr, me_r + d), (1, me_r >= d, me_r - d)):
            pl.when(cond)(
                lambda side=side, r=r: pl.semaphore_signal(
                    token.at[s, side], inc=1, device_id=(me_l, r), device_id_type=MESH
                )
            )

    def token_wait(s):
        d = reach[s]
        for side, cond in ((0, me_r >= d), (1, me_r + d < nr)):
            pl.when(cond)(lambda side=side: pl.semaphore_wait(token.at[s, side], 1))

    def tokens(s):
        if s < len(reach):
            token_wait(s)
            if s + 1 < len(reach):
                token_send(s + 1)

    RP = 8
    RM = RP + na - 1

    def edges(k):
        here = q.at[k]
        own = psi if k == 0 else here.at[1 : na + 1, 1 : nb + 1]

        def rows(ref, h):
            lead = (slice(None),) * (len(ref.shape) - 2)
            return ref.at[lead + (pl.ds(h * half, half),)]

        out = {
            "U2": (has_hi_l, has_lo_l, own.at[na - 1, 1:nb], here.at[0, 2 : nb + 1], (hi_l, me_r), 0, 0),
            "U1": (both(up_dn, no(via_hi)), dn_up, own.at[na - 1, 0], here.at[0, nb + 1], (hi_l, lo_r), 1, 1),
            "D1": (both(has_lo_l, no(via_lo)), has_hi_l, own.at[0, 0 : nb - 1], here.at[na + 1, 1:nb], (lo_l, me_r), 2, 2),
            "D2": (dn_up, up_dn, own.at[0, nb - 1], here.at[na + 1, 0], (lo_l, hi_r), 3, 3),
        }
        for h in range(2):
            up, dn = rows(stage_up.at[k], h), rows(stage_dn.at[k], h)
            out[f"U1h{h}"] = (via_hi, relay_up, rows(own.at[na - 1, 0], h), up, (me_l + 2, me_r), 4 + h, 4 + h)
            out[f"D1h{h}"] = (via_lo, relay_dn, rows(own.at[0, 0 : nb - 1], h), dn, (me_l - 2, me_r), 6 + h, 6 + h)
            out[f"FU{h}"] = (relay_up, None, up, rows(here.at[0, nb + 1], h), (lo_l, lo_r), RM + na - 1 + h, 1)
            out[f"FD{h}"] = (relay_dn, None, dn, rows(here.at[na + 1, 1:nb], h), (hi_l, me_r), RM + na + 1 + h, 2)
        for i in range(1, na):
            n = RP + i - 1
            out[f"RP{i}"] = (has_lo_r, has_hi_r, own.at[i - 1, 0], here.at[i, nb + 1], (me_l, lo_r), n, n)
            n = RM + i - 1
            out[f"RM{i + 1}"] = (has_hi_r, has_lo_r, own.at[i, nb - 1], here.at[i + 1, 0], (me_l, hi_r), n, n)
        return out

    links = [edges(k) for k in range(ITERS)]

    def copy(k, name):
        _, _, src, dst, target, ssem, rsem = links[k][name]
        return pltpu.make_async_remote_copy(
            src_ref=src, dst_ref=dst,
            send_sem=send_sem.at[k, ssem], recv_sem=recv_sem.at[k, rsem],
            device_id=target, device_id_type=MESH,
        )

    def send(k, *names, when=None):
        if k < ITERS:
            for name in names:
                cond = links[k][name][0]
                cond = cond if when is None else both(cond, when)
                pl.when(cond)(lambda name=name: copy(k, name).start())

    def receive(k, *names, when=None):
        for name in names:
            cond = links[k][name][1]
            cond = cond if when is None else both(cond, when)
            pl.when(cond)(lambda name=name: copy(k, name).wait_recv())

    pl.semaphore_wait(barrier, partners)
    send(0, "U1h0", "D1h0", "U1h1", "D1h1", "U1", when=odd)
    send(0, "D1h0", "D1h1", when=even)
    send(0, "D1", when=odd)
    send(0, "U2", when=even)
    send(0, f"RP{na - 1}", "RM2")
    send(0, "U2", when=odd)
    send(0, "D2", "D1", when=even)
    rest_rp = [f"RP{i}" for i in range(na - 2, 0, -1)]
    rest_rm = [f"RM{i}" for i in range(3, na + 1)]
    send(0, *[name for pair in zip(rest_rp, rest_rm) for name in pair])
    token_send(0) if reach else None

    def clear(missing, slots):
        @pl.when(no(missing))
        def _():
            for k in range(ITERS):
                for i, j in slots:
                    q[k, i, j] = jnp.zeros((size, size), q.dtype)

    def row(i):
        return jnp.where(odd, i, na + 1 - i)

    def col(j):
        return jnp.where(odd, j, nb + 1 - j)

    def shift(t):
        return 0 if t < DIAG else (1 if t < DIAG + HOPS else -1)

    def which(t):
        if t < DIAG:
            return t
        other = t + HOPS if t < DIAG + HOPS else t - HOPS
        return jnp.where(odd, t, other)

    def block(k, i, j):
        return q[k, row(i), col(j)]

    def term(k, i, j, t):
        source = block(k, i - shift(t), j + shift(t))
        inner = jnp.dot(left[row(i) - 1, which(t)], source, preferred_element_type=jnp.float32)
        return jnp.dot(
            inner.astype(jnp.bfloat16), right_t[col(j) - 1, which(t)],
            preferred_element_type=jnp.float32,
        )

    def is_local(i, j, t):
        return 1 <= i - shift(t) <= na and 1 <= j + shift(t) <= nb

    every = [(i, j) for i in range(1, na + 1) for j in range(1, nb + 1)]
    last = (1, nb)

    def begin(k, i, j, skip=None, only=False, fresh=True):
        if fresh:
            total = (energies[col(j) - 1, row(i) - 1] - SHIFT) * block(k, i, j).astype(jnp.float32)
        else:
            total = acc[k % 2, row(i) - 1, col(j) - 1]
        for t in range(TERMS):
            if only and t >= DIAG or not fresh and t < DIAG:
                continue
            if is_local(i, j, t) and (i - shift(t), j + shift(t)) != skip:
                total += term(k, i, j, t)
        acc[k % 2, row(i) - 1, col(j) - 1] = total

    def add(x, y, a, b):
        part = jnp.sum(x * y, axis=0, keepdims=True)
        at = pl.ds(gram_row(a, b), 1)
        for lane in range(0, size, 128):
            local[at, :] += part[:, lane : lane + 128]

    def grams(k, blocks):
        for i, j in blocks:
            new = block(k, i, j).astype(jnp.float32)
            for a in range(k + 1):
                add(block(a, i, j).astype(jnp.float32), new, a, k)

    def finish(k, i, j):
        total = acc[k % 2, row(i) - 1, col(j) - 1]
        for t in range(DIAG, TERMS):
            if not is_local(i, j, t):
                total += term(k, i, j, t)
        if k + 1 < ITERS:
            q[k + 1, row(i), col(j)] = total.astype(jnp.bfloat16)
        else:
            acc[k % 2, row(i) - 1, col(j) - 1] = total
            for a in range(ITERS):
                add(block(a, i, j).astype(jnp.float32), total, a, ITERS)
            add(total, total, ITERS, ITERS)

    def everyone(slots, ssem, rsem):
        def to(n):
            at = lax.rem(me + n, parts)
            return pltpu.make_async_remote_copy(
                src_ref=slots.at[me], dst_ref=slots.at[me], send_sem=ssem, recv_sem=rsem,
                device_id=(at // nr, lax.rem(at, nr)), device_id_type=MESH,
            )

        def begin():
            lax.fori_loop(1, parts, lambda n, c: (to(n).start(), c)[1], 0)

        whole = pltpu.make_async_remote_copy(
            src_ref=slots.at[0 : parts - 1], dst_ref=slots.at[0 : parts - 1],
            send_sem=ssem, recv_sem=rsem, device_id=(me_l, me_r), device_id_type=MESH,
        )
        return begin, whole

    def packed(first, size):
        totals = jnp.sum(local[...], axis=1, keepdims=True)
        place = lax.broadcasted_iota(jnp.int32, local.shape, 0)
        lanes = lax.broadcasted_iota(jnp.int32, local.shape, 1)
        return jnp.sum(jnp.where(place == lanes, totals, 0.0), axis=0, keepdims=True)

    early_begin, early_whole = everyone(early, esend, erecv)
    late_begin, late_whole = everyone(late, lsend, lrecv)

    def forward(k, h):
        receive(k, f"U1h{h}", f"D1h{h}")
        send(k, f"FU{h}", f"FD{h}")

    loads[1].wait()
    for j in range(nb):
        for t in range(TERMS):
            right_t[j, t] = right[j, t].T
    for load in loads[:1] + loads[2:]:
        load.wait()
    forward(0, 0)
    for j in range(1, nb):
        begin(0, 1, j)
    forward(0, 1)
    send(0, "D2", when=odd)
    send(0, "U1", when=even)
    clear(has_lo_l, [(0, j) for j in range(2, nb + 1)])
    clear(dn_up, [(0, nb + 1)])
    clear(has_hi_l, [(na + 1, j) for j in range(1, nb)])
    clear(up_dn, [(na + 1, 0)])
    clear(has_hi_r, [(i, nb + 1) for i in range(1, na)])
    clear(has_lo_r, [(i, 0) for i in range(2, na + 1)])
    local[...] = jnp.zeros(local.shape, jnp.float32)
    for k in range(ITERS):
        n = k + 1

        receive(k, "U2", "RM2", when=odd)
        receive(k, "D1", f"RP{na - 1}", when=even)
        for j in range(1, nb):
            finish(k, 1, j)
        send(n, "D1", "RP1", when=odd)
        send(n, "U2", f"RM{na}", when=even)

        if k == 0:
            for i, j in every:
                if i > 1 or j == nb:
                    begin(0, i, j)
        receive(k, *rest_rp, *rest_rm)
        inner = [(2, nb)] if na > 2 else []
        if na > 2:
            inner.append((na - 1, 1))
        for i, j in inner:
            finish(k, i, j)
        if na > 2:
            send(n, f"RP{na - 1}", "RM2")
        for i in range(2, na):
            for j in range(1, nb + 1):
                if (i, j) not in inner:
                    finish(k, i, j)
        send(n, *[f"RP{i}" for i in range(2, na - 1)], *[f"RM{i}" for i in range(3, na)])
        if k == 1:
            tokens(1)
        if n < ITERS:
            for i in range(2, na):
                for j in range(1, nb + 1):
                    begin(n, i, j, only=True)
            grams(n, [(i, j) for i in range(1, na) for j in range(1, nb + 1) if (i, j) != last])

        if k == 0:
            grams(0, every)
        receive(k, "D1", f"RP{na - 1}", when=odd)
        receive(k, "U2", "RM2", when=even)
        for j in range(2, nb + 1):
            finish(k, na, j)
        send(n, "U2", f"RM{na}", when=odd)
        send(n, "D1h0", "D1h1", "D1", "RP1", when=even)

        receive(k, "D2", when=odd)
        receive(k, "U1", when=even)
        finish(k, na, 1)
        send(n, "U1h0", "U1h1", "U1", when=odd)
        send(n, "D2", when=even)

        if n < ITERS:
            for i, j in every:
                if 1 < i < na:
                    begin(n, i, j, skip=last, fresh=False)
                elif (i, j) != last:
                    begin(n, i, j, skip=last)
            grams(n, [(na, j) for j in range(1, nb + 1)])

        receive(k, "U1", when=odd)
        receive(k, "D2", when=even)
        finish(k, *last)
        if n == ITERS - 1:
            for s in range(2, len(reach)):
                tokens(s)
            grams(n, [last])
            early[me] = packed(0, 0)
            early_begin()
        send(n, "D2", when=odd)
        send(n, "U1", when=even)
        if n < ITERS:
            for h in range(2):
                forward(n, h)
            begin(n, *last)
            if nb > 1:
                acc[n % 2, row(2) - 1, col(nb - 1) - 1] += term(n, 2, nb - 1, DIAG)
            if n < ITERS - 1:
                grams(n, [last])
        if k == 0:
            tokens(0)

    late[me] = packed(0, 0)
    late_begin()

    def plus(x, y):
        return y if x is None else (x if y is None else x + y)

    def scaled(s, x):
        return [None if part is None else s * part for part in x]

    def combine(*lists):
        return [functools.reduce(plus, parts) for parts in zip(*lists)]

    def product(x, y):
        total = jnp.zeros((1, 1), jnp.float32)
        for i in range(ITERS):
            for j in range(ITERS):
                if x[i] is not None and y[j] is not None:
                    at = gram_row(min(i, j), max(i, j))
                    total = total + x[i] * y[j] * sums[:, at : at + 1]
        return total

    early_whole.wait_recv()
    sums = jnp.sum(early[...], axis=0) * count
    vec = [lax.rsqrt(sums[:, 0:1] + eps)] + [None] * ITERS
    previous = None
    theta = []
    for k in range(ITERS):
        image = combine([None] + vec[:-1], scaled(SHIFT, vec))
        resid = image
        if k > 0:
            coef = jnp.full((1, 1), coef_num[k - 1].astype(jnp.float32)) / jnp.full(
                (1, 1), coef_den[k - 1].astype(jnp.float32)
            )
            resid = combine(resid, scaled(-coef, previous))
        if k + 1 == ITERS:
            break
        theta.append(product(vec, image))
        resid = combine(resid, scaled(-theta[k], vec))
        previous = vec
        vec = scaled(lax.rsqrt(product(resid, resid) + eps), resid)

    for i in range(na):
        for j in range(nb):
            new = acc[(ITERS - 1) % 2, i, j] * resid[ITERS]
            old = None
            for a in range(ITERS):
                part = q[a, i + 1, j + 1].astype(jnp.float32)
                new += part * resid[a]
                old = plus(old, part * vec[a])
            ahead[i, j] = new
            prior[i, j] = old

    theta_known = product(vec, image)
    both_known = product(resid, vec)
    new_known = product(resid, resid)
    old_known = product(vec, vec)
    early_whole.wait_send()
    for k in range(ITERS):
        for name, link in links[k].items():
            pl.when(link[0])(lambda k=k, name=name: copy(k, name).wait_send())

    late_whole.wait_recv()
    sums = jnp.sum(late[...], axis=0) * count

    def cross(x):
        total = jnp.zeros((1, 1), jnp.float32)
        for a in range(ITERS):
            at = gram_row(a, ITERS)
            total = total + x[a] * sums[:, at : at + 1]
        return total

    at = gram_row(ITERS, ITERS)
    top = resid[ITERS]
    with_vec = top * cross(vec)
    theta.append(theta_known + with_vec)
    overlap = both_known + with_vec
    square = new_known + top * (2.0 * cross(resid) + top * sums[:, at : at + 1])
    norm = square - theta[-1] * (2.0 * overlap - theta[-1] * old_known)
    scale = lax.rsqrt(norm + eps)
    values = [scale, scale * theta[-1]] + theta
    for n, value in enumerate(values):
        scalars[n : n + 1, :] = jnp.broadcast_to(value, (1, scalars.shape[1]))
    late_whole.wait_send()


def close(ahead, prior, scalars, out_hbm, ritz, out_v, sem):
    na, nb = ahead.shape[:2]
    scale, drop = scalars[0:1, 0:1], scalars[1:2, 0:1]
    stores = []
    for i in range(na):
        for j in range(nb):
            out_v[i, j] = (ahead[i, j] * scale - prior[i, j] * drop).astype(jnp.bfloat16)
            stores.append(pltpu.make_async_copy(out_v.at[i, j], out_hbm.at[i, j], sem.at[i, j]))
            stores[-1].start()
    for k in range(ITERS):
        ritz[k] = scalars[2 + k, 0]
    for store in stores:
        store.wait()


def per_device(nl, nr, psi, left_env, right_env, energies, coef_num, coef_den):
    na, nb, size, _ = psi.shape
    count = 1.0 / float(psi.size * nl * nr)
    hbm = pl.BlockSpec(memory_space=pltpu.HBM)
    smem = pl.BlockSpec(memory_space=pltpu.SMEM)
    vmem = pl.BlockSpec(memory_space=pltpu.VMEM)
    dma = pltpu.SemaphoreType.DMA
    flows = 12 + 2 * (na - 1)
    ahead, prior, scalars = pl.pallas_call(
        functools.partial(kernel, nl, nr, count),
        out_shape=(
            pltpu.VMEM(psi.shape, jnp.float32),
            pltpu.VMEM(psi.shape, jnp.float32),
            pltpu.VMEM((8, 128), jnp.float32),
        ),
        in_specs=[hbm] * 6,
        out_specs=(vmem, vmem, vmem),
        scratch_shapes=[
            pltpu.SMEM((nb, na), jnp.float32),
            pltpu.SMEM(coef_num.shape, jnp.int32),
            pltpu.SMEM(coef_den.shape, jnp.int32),
            pltpu.VMEM((ITERS, na + 2, nb + 2, size, size), jnp.bfloat16),
            pltpu.VMEM((ITERS, size, size), jnp.bfloat16),
            pltpu.VMEM((ITERS, nb - 1, size, size), jnp.bfloat16),
            pltpu.VMEM(left_env.shape, jnp.bfloat16),
            pltpu.VMEM(right_env.shape, jnp.bfloat16),
            pltpu.VMEM(right_env.shape, jnp.bfloat16),
            pltpu.VMEM((2,) + psi.shape, jnp.float32),
            pltpu.VMEM((GRAMS, 128), jnp.float32),
            pltpu.VMEM((nl * nr, 1, 128), jnp.float32),
            pltpu.VMEM((nl * nr, 1, 128), jnp.float32),
            dma((6,)),
            dma((ITERS, flows)),
            dma((ITERS, flows)),
            pltpu.SemaphoreType.REGULAR((max(1, len(spans(nr))), 2)),
            dma, dma, dma, dma,
        ],
        compiler_params=pltpu.CompilerParams(
            collective_id=0, has_side_effects=True, vmem_limit_bytes=60000000
        ),
    )(psi, left_env, right_env, energies.T, coef_num, coef_den)
    return pl.pallas_call(
        close,
        out_shape=(
            jax.ShapeDtypeStruct(psi.shape, jnp.bfloat16),
            jax.ShapeDtypeStruct((ITERS,), jnp.float32),
        ),
        in_specs=[vmem] * 3,
        out_specs=(hbm, smem),
        scratch_shapes=[pltpu.VMEM(psi.shape, jnp.bfloat16), dma((na, nb))],
        compiler_params=pltpu.CompilerParams(vmem_limit_bytes=8000000),
    )(ahead, prior, scalars)


def solution(mesh):
    in_specs = (
        P("lsec", "rsec", None, None),
        P("lsec", None, None, None),
        P("rsec", None, None, None),
        P("lsec", "rsec"),
        P(),
        P(),
    )
    out_specs = (P("lsec", "rsec", None, None), P())
    body = functools.partial(per_device, mesh.shape["lsec"], mesh.shape["rsec"])
    return jax.shard_map(
        body, mesh=mesh, in_specs=in_specs, out_specs=out_specs, check_vma=False
    )
```
